32 devices in a mesh: dp: 4 (over z), tensor: 8 (over y, x, core).
Axes of the slice: x: 2, y: 2, z: 4, core: 2. Of those that a mesh axis runs over, the one named last changes fastest.
Arguments:
- teacher_hidden: bfloat16 [64, 5120], P('dp', 'tensor'), may hold values from -200 to 200
- student_hidden: bfloat16 [64, 4096], P('dp', 'tensor'), may hold values from -8 to 8
- teacher_head: bfloat16 [5120, 8192], P(None, ('dp', 'tensor')), may hold values from -6 to 6
- student_head: bfloat16 [4096, 8192], P(None, ('dp', 'tensor')), may hold values from -6 to 6
- teacher_gain: float32 [5120], replicated, may hold values from 0.5 to 1.5
- lengths: int32 [8], replicated, may hold values from 1 to 8, as said below
- student_row: int32 [64], replicated, may hold values from 0 to 63, as said below
- targets: int32 [64], replicated, may hold values from 0 to 8191
Outputs:
- grad_logits: bfloat16 [64, 8192], P(None, ('dp', 'tensor'))
- divergence: float32 [64], P('dp')
- log_ratio: float32 [64], P('dp')
The draws below stay inside these ranges and needn't reach their ends.
Inputs may be any that keep to these rules, and one draw needn't show every extreme that they name: The lengths of the 2 responses of one index of dp sum to at most 8, and to exactly 8 on some index. `student_row`: a permutation: every row of student_hidden is named once.
All inputs are finite; a program needn't handle non-finite values.
Results may differ from the reference program's by a relative error of at most 0.01095.
Values may be sent and summed in bfloat16 or wider, within the bound.
A program may use at most 64 MiB of HBM per device.

```python
import math
import jax
import jax.numpy as jnp
import numpy as np
from jax import lax

DT = 5120
DS = 4096
SLOT = 8
SEQ_DEV = 2
LIVE_DEV = 8
SEQS = 8
TOKENS = 64
VOCAB = 8192


paired_count = 6


planted_score = 200.0


def pairing(key):
    base = jax.random.fold_in(key, 7)
    keys = jax.random.split(base, 6)
    token_rows = jax.random.randint(keys[0], (paired_count,), 0, TOKENS)
    columns = jax.random.randint(keys[1], (paired_count,), 0, VOCAB - 1)
    strength = jax.random.uniform(keys[2], (paired_count,), jnp.float32, 0.6, 1.15).at[0].set(1.15)
    teacher_gap = jax.random.uniform(keys[3], (paired_count,), jnp.float32, 1.0, 3.0)
    student_gap = jax.random.uniform(keys[4], (paired_count,), jnp.float32, 1.0, 3.0)
    order = jax.random.permutation(keys[5], TOKENS).astype(jnp.int32)
    return (token_rows, columns, strength, teacher_gap, student_gap, order)


def teacher_values(key):
    inner = jax.random.fold_in(key, 21)
    return jnp.clip(jax.random.normal(inner, (TOKENS, DT), jnp.float32), -6.0, 6.0)


def student_values(key):
    inner = jax.random.fold_in(key, 31)
    return jnp.clip(jax.random.normal(inner, (TOKENS, DS), jnp.float32), -6.0, 6.0)


def base_head(key, width, depth):
    return jnp.clip(jax.random.normal(key, (depth, VOCAB), jnp.float32), -6.0, 6.0) * width


def draw_teacher_hidden(key, part):
    return teacher_values(key).astype(jnp.bfloat16)


def draw_student_hidden(key, part):
    return student_values(key).astype(jnp.bfloat16)


def draw_teacher_head(key, part):
    width = 3.0 / math.sqrt(DT)
    head = base_head(jax.random.fold_in(key, 22), width, DT)
    token_rows, columns, strength, teacher_gap, student_gap, order = pairing(key)
    chosen = teacher_values(key)[token_rows]
    unit_rows = chosen * lax.rsqrt(jnp.mean(chosen * chosen, axis=1, keepdims=True))
    nominal = planted_score * strength
    column = unit_rows * (nominal / DT)[:, None]
    second = column * (1.0 - teacher_gap / nominal)[:, None]
    head = head.at[:, columns].set(column.T)
    head = head.at[:, columns + 1].set(second.T)
    return head.astype(jnp.bfloat16)


def draw_student_head(key, part):
    width = 3.0 / math.sqrt(DS)
    head = base_head(jax.random.fold_in(key, 32), width, DS)
    token_rows, columns, strength, teacher_gap, student_gap, order = pairing(key)
    chosen = student_values(key)[order[token_rows]]
    nominal = planted_score * strength
    column = chosen / jnp.mean(chosen * chosen, axis=1, keepdims=True) * (nominal / DS)[:, None]
    second = column * (1.0 - student_gap / nominal)[:, None]
    head = head.at[:, columns].set(column.T)
    head = head.at[:, columns + 1].set(second.T)
    return head.astype(jnp.bfloat16)


def draw_student_row(key, part):
    return pairing(key)[5]


def draw_lengths(key, part):
    inner = jax.random.fold_in(key, 41)
    keys = jax.random.split(inner, 2)
    groups = SEQS // SEQ_DEV
    raw_lengths = jax.random.randint(keys[0], (groups, SEQ_DEV), 1, SLOT + 1)
    busiest = jax.random.randint(keys[1], (), 0, groups)
    raw_lengths = jnp.where(jnp.arange(groups)[:, None] == busiest, SLOT, raw_lengths)
    used = jnp.zeros((groups,), jnp.int32)
    columns = []
    for number in range(SEQ_DEV):
        room = LIVE_DEV - (SEQ_DEV - 1 - number) - used
        length_now = jnp.minimum(raw_lengths[:, number], room)
        used = used + length_now
        columns.append(length_now)
    return jnp.stack(columns, axis=1).reshape(SEQS).astype(jnp.int32)


def set_ends(drawn, key, smallest, largest):
    extent = drawn.shape
    index_at = [jax.random.randint(jax.random.fold_in(key, axis), (), 0, extent[axis]) for axis in range(len(extent))]
    drawn = drawn.at[tuple(index_at)].set(smallest)
    longest = extent.index(max(extent))
    index_at[longest] = (index_at[longest] + 1) % extent[longest]
    return drawn.at[tuple(index_at)].set(largest)


def cumulative_ranks(number_of, slope):
    loads = [(1 << 20) // math.isqrt(grade ** slope) + 1 for grade in range(1, number_of + 1)]
    scale = 1 + sum(loads) // (1 << 30)
    return np.cumsum(np.array([max(1, weight // scale) for weight in loads]))


def skewed_ids(stream_key, dims, number_of, slope):
    listing = cumulative_ranks(number_of, slope)
    lot = jax.random.randint(jax.random.fold_in(stream_key, 1), dims, 0, int(listing[number_of - 1]))
    standing = jnp.searchsorted(jnp.asarray(listing, jnp.int32), lot, side="right")
    return jax.random.permutation(jax.random.fold_in(stream_key, 2), number_of)[standing].astype(jnp.int32)


def setup_inputs(seed: int = 0) -> dict:
    arg_keys = jax.random.split(jax.random.key(seed), 9)
    teacher_hidden = draw_teacher_hidden(jax.random.fold_in(arg_keys[8], 71), 0)
    student_hidden = draw_student_hidden(jax.random.fold_in(arg_keys[8], 71), 0)
    teacher_head = draw_teacher_head(jax.random.fold_in(arg_keys[8], 71), 0)
    student_head = draw_student_head(jax.random.fold_in(arg_keys[8], 71), 0)
    teacher_gain = jnp.clip(1.0 + 0.1 * jax.random.normal(arg_keys[4], (DT,), jnp.float32), 0.5, 1.5)
    lengths = draw_lengths(jax.random.fold_in(arg_keys[8], 71), 0)
    student_row = draw_student_row(jax.random.fold_in(arg_keys[8], 71), 0)
    targets = set_ends(skewed_ids(arg_keys[7], (TOKENS,), VOCAB, 2), jax.random.fold_in(arg_keys[7], 3), 0, VOCAB - 1).astype(jnp.int32)
    return {"teacher_hidden": teacher_hidden, "student_hidden": student_hidden, "teacher_head": teacher_head, "student_head": student_head, "teacher_gain": teacher_gain, "lengths": lengths, "student_row": student_row, "targets": targets}


def reference(teacher_hidden, student_hidden, teacher_head, student_head, teacher_gain, lengths, student_row, targets):
    token_count = teacher_hidden.shape[0]
    token_ids = jnp.arange(token_count, dtype=jnp.int32)
    live_mask = (token_ids % SLOT < lengths[token_ids // SLOT]).astype(jnp.float32)
    hidden_rows = teacher_hidden.astype(jnp.float32)
    row_scale = lax.rsqrt(lax.optimization_barrier(jnp.mean(hidden_rows * hidden_rows, axis=1, keepdims=True)) + 1e-06)
    normed = (hidden_rows * row_scale * teacher_gain[None, :]).astype(jnp.bfloat16)
    teacher_logits = jnp.dot(normed, teacher_head, preferred_element_type=jnp.float32)
    student_logits = jnp.dot(student_hidden[student_row], student_head, preferred_element_type=jnp.float32)
    teacher_logp = teacher_logits - jax.nn.logsumexp(teacher_logits, axis=1)[:, None]
    student_logp = student_logits - jax.nn.logsumexp(student_logits, axis=1)[:, None]
    student_prob = jnp.exp(student_logp)
    kl_raw = lax.optimization_barrier(jnp.sum(student_prob * (student_logp - teacher_logp), axis=1))
    picked_student = jnp.take_along_axis(student_logp, targets[:, None], axis=1)[:, 0]
    picked_teacher = jnp.take_along_axis(teacher_logp, targets[:, None], axis=1)[:, 0]
    log_ratio = live_mask * (picked_student - picked_teacher)
    gradient = live_mask[:, None] * student_prob * (student_logp - teacher_logp - kl_raw[:, None])
    return (gradient.astype(jnp.bfloat16), live_mask * kl_raw, log_ratio)
```

```python
import functools

import jax
import jax.numpy as jnp
from jax import lax
from jax.experimental import pallas as pl
from jax.experimental.pallas import tpu as pltpu
from jax.sharding import PartitionSpec as P

LIVE = 8
MESH = pl.DeviceIdType.MESH


def kernel(
    n_dp,
    n_t,
    th_hbm,
    sh_hbm,
    thead_hbm,
    shead_hbm,
    gain_hbm,
    len_hbm,
    srow_hbm,
    tgt_hbm,
    out_ref,
    div_ref,
    ratio_ref,
    th,
    thead,
    shead,
    gain,
    lens,
    srow,
    tgt,
    tg,
    sz,
    sg,
    mine,
    stats,
    local_sem,
    zt_send,
    zt_recv,
    zs_send,
    zs_recv,
    xt_send,
    xt_recv,
    xs_send,
    xs_recv,
    pt_send,
    pt_recv,
    ps_send,
    ps_recv,
    st_send,
    st_recv,
):
    f32, bf16 = jnp.float32, jnp.bfloat16
    d = lax.axis_index("dp")
    t = lax.axis_index("tensor")
    half = n_t // 2
    chip, core = t // 2, t % 2
    partner = chip * 2 + 1 - core
    local_tokens, width_t = th_hbm.shape
    width_s = sh_hbm.shape[1]
    tokens = local_tokens * n_dp
    seqs = lens.shape[0]
    seq_dev = seqs // n_dp
    slot = tokens // seqs
    vocab = thead.shape[1]
    rows = n_dp * LIVE
    lanes = 4 * rows
    n_dev = n_dp * n_t

    local = [
        pltpu.make_async_copy(src, dst, local_sem.at[i])
        for i, (src, dst) in enumerate(
            [
                (len_hbm, lens),
                (th_hbm, th),
                (sh_hbm, sz.at[d]),
                (srow_hbm, srow),
                (tgt_hbm, tgt),
                (gain_hbm, gain),
                (shead_hbm, shead),
                (thead_hbm, thead),
            ]
        )
    ]
    for copy in local:
        copy.start()

    def dp_peer(k):
        return lax.rem(d + k, n_dp)

    def chip_peer(k):
        return lax.rem(chip + k, half) * 2 + core

    barrier = pltpu.get_barrier_semaphore()
    for k in range(1, n_dp):
        pl.semaphore_signal(barrier, inc=1, device_id=(dp_peer(k), t), device_id_type=MESH)
    for k in range(1, half):
        pl.semaphore_signal(barrier, inc=1, device_id=(d, chip_peer(k)), device_id_type=MESH)
    pl.semaphore_signal(barrier, inc=1, device_id=(d, partner), device_id_type=MESH)

    local[0].wait()
    lane = lax.broadcasted_iota(jnp.int32, (1, local_tokens), 1)
    own_slot = jnp.full((1, local_tokens), -1, jnp.int32)
    offset = jnp.int32(0)
    for q in range(seq_dev):
        length = lens[d * seq_dev + q]
        pos = lane - q * slot
        own_slot = jnp.where((pos >= 0) & (pos < length), pos + offset, own_slot)
        offset = offset + length
    own_hit = lax.broadcasted_iota(jnp.int32, (LIVE, local_tokens), 0) == own_slot
    local[1].wait()
    tg[t, d] = jnp.dot(
        jnp.where(own_hit, 1.0, 0.0).astype(bf16), th[...], preferred_element_type=f32
    ).astype(bf16)
    local[2].wait()

    pl.semaphore_wait(barrier, n_dp - 1 + half - 1 + 1)

    def remote(src, dst, send, recv, device):
        return pltpu.make_async_remote_copy(
            src_ref=src, dst_ref=dst, send_sem=send, recv_sem=recv, device_id=device, device_id_type=MESH
        )

    started = []
    z_t, z_s = [], []
    for k in range(1, n_dp):
        z_t.append(
            remote(tg.at[t, d], tg.at[t, d], zt_send.at[k], zt_recv.at[k], (dp_peer(k), t))
        )
        z_s.append(remote(sz.at[d], sz.at[d], zs_send.at[k], zs_recv.at[k], (dp_peer(k), t)))
    for copy in z_t + z_s:
        copy.start()
    started += z_t + z_s

    local[3].wait()
    local[4].wait()
    token = lax.broadcasted_iota(jnp.int32, (1, tokens), 1)
    slot_of = jnp.full((1, tokens), -1, jnp.int32)
    for s in range(seqs):
        if s % seq_dev == 0:
            offset = jnp.int32(s // seq_dev * LIVE)
        length = lens[s]
        pos = token - s * slot
        slot_of = jnp.where((pos >= 0) & (pos < length), pos + offset, slot_of)
        offset = offset + length
    row = lax.broadcasted_iota(jnp.int32, (rows, tokens), 0)
    hit = row == slot_of
    hit_bf16 = jnp.where(hit, 1.0, 0.0).astype(bf16)
    source = jnp.sum(jnp.where(hit, srow[...].astype(f32), 0.0), axis=1, keepdims=True)
    wanted = jnp.sum(jnp.where(hit, tgt[...].astype(f32), 0.0), axis=1, keepdims=True)
    pick = lax.broadcasted_iota(jnp.int32, (rows, tokens), 1) == source.astype(jnp.int32)
    pick_bf16 = jnp.where(pick, 1.0, 0.0).astype(bf16)

    for copy in z_t:
        copy.wait_recv()
    x_t = [
        remote(tg.at[t], tg.at[t], xt_send.at[k], xt_recv.at[k], (d, chip_peer(k)))
        for k in range(1, half)
    ]
    p_t = [remote(tg.at[t], tg.at[t], pt_send.at[0], pt_recv.at[0], (d, partner))]
    for copy in x_t + p_t:
        copy.start()

    for copy in z_s:
        copy.wait_recv()
    everyone = sz[...].reshape(tokens, width_s)
    sg[t] = jnp.dot(pick_bf16, everyone, preferred_element_type=f32).astype(bf16)
    x_s = [
        remote(sg.at[t], sg.at[t], xs_send.at[k], xs_recv.at[k], (d, chip_peer(k)))
        for k in range(1, half)
    ]
    p_s = [remote(sg.at[t], sg.at[t], ps_send.at[0], ps_recv.at[0], (d, partner))]
    for copy in x_s + p_s:
        copy.start()

    for copy in local[5:]:
        copy.wait()

    square = jnp.zeros((rows, 1), f32)
    acc_t = jnp.zeros((2 * rows, vocab), f32)
    acc_s = jnp.zeros((rows, vocab), f32)

    def add(which, square, acc_t, acc_s):
        x = tg[which].astype(f32).reshape(rows, width_t)
        square = square + jnp.sum(x * x, axis=1, keepdims=True)
        x = x * gain[which]
        high = x.astype(bf16)
        low = (x - high.astype(f32)).astype(bf16)
        at_t = pl.ds(pl.multiple_of(which * width_t, width_t), width_t)
        at_s = pl.ds(pl.multiple_of(which * width_s, width_s), width_s)
        acc_t = acc_t + jnp.dot(
            jnp.concatenate([high, low], axis=0), thead[at_t, :], preferred_element_type=f32
        )
        acc_s = acc_s + jnp.dot(sg[which], shead[at_s, :], preferred_element_type=f32)
        return square, acc_t, acc_s

    sums = add(t, square, acc_t, acc_s)
    for k in range(1, half):
        origin = lax.rem(chip - k + half, half) * 2 + core
        x_t[k - 1].wait_recv()
        copy = remote(tg.at[origin], tg.at[origin], pt_send.at[k], pt_recv.at[k], (d, partner))
        copy.start()
        p_t.append(copy)
        x_s[k - 1].wait_recv()
        copy = remote(sg.at[origin], sg.at[origin], ps_send.at[k], ps_recv.at[k], (d, partner))
        copy.start()
        p_s.append(copy)
        sums = add(origin, *sums)
    for k in range(half):
        origin = lax.rem(chip - k + half, half) * 2 + 1 - core
        p_t[k].wait_recv()
        p_s[k].wait_recv()
        sums = add(origin, *sums)
    square, acc_t, acc_s = sums
    started += x_t + x_s + p_t + p_s

    scale = lax.rsqrt(square / (width_t * n_t) + 1e-06)
    logits_t = (acc_t[:rows] + acc_t[rows:]) * scale
    gap = acc_s - logits_t
    max_t = jnp.max(logits_t, axis=1, keepdims=True)
    max_s = jnp.max(acc_s, axis=1, keepdims=True)
    sum_t = jnp.sum(jnp.exp(logits_t - max_t), axis=1, keepdims=True)
    exp_s = jnp.exp(acc_s - max_s)
    sum_s = jnp.sum(exp_s, axis=1, keepdims=True)
    cross = jnp.sum(exp_s * gap, axis=1, keepdims=True) / sum_s
    me = d * n_t + t
    column = lax.broadcasted_iota(jnp.int32, (rows, vocab), 1) + me * vocab
    chosen = jnp.sum(
        jnp.where(column == wanted.astype(jnp.int32), gap, 0.0), axis=1, keepdims=True
    )

    place = lax.broadcasted_iota(jnp.int32, (rows, lanes), 1) - lax.broadcasted_iota(
        jnp.int32, (rows, lanes), 0
    )
    packed = jnp.zeros((rows, lanes), f32)
    for i, value in enumerate((max_t + jnp.log(sum_t), max_s + jnp.log(sum_s), cross, chosen)):
        packed = jnp.where(place == i * rows, value, packed)
    mine[...] = jnp.sum(packed, axis=0, keepdims=True)
    stats[me] = mine[...]

    def stat(k):
        peer = lax.rem(me + k, n_dev)
        return remote(
            mine, stats.at[me], st_send.at[k], st_recv.at[k], (peer // n_t, lax.rem(peer, n_t))
        )

    def start(k, carry):
        stat(k).start()
        return carry

    def finish(k, carry):
        stat(k).wait()
        return carry

    lax.fori_loop(1, n_dev, start, 0)
    for copy in started:
        copy.wait_send()
    lax.fori_loop(1, n_dev, finish, 0)

    table = stats[...].reshape(n_dev, lanes)
    top = jnp.max(table, axis=0, keepdims=True)
    weight = jnp.exp(table - top)
    total = jnp.sum(weight, axis=0, keepdims=True)
    lse = top + jnp.log(total)
    moved = pltpu.roll(weight, rows, 1)
    mean_gap = jnp.sum(table * moved, axis=0, keepdims=True) / jnp.sum(moved, axis=0, keepdims=True)
    target_gap = jnp.sum(table, axis=0, keepdims=True)

    def per_slot(value, i):
        return jnp.sum(jnp.where(place == i * rows, value, 0.0), axis=1, keepdims=True)

    lse_t, lse_s = per_slot(lse, 0), per_slot(lse, 1)
    mean = per_slot(mean_gap, 2)
    ratio = per_slot(target_gap, 3) - lse_s + lse_t
    kl = mean - lse_s + lse_t
    gradient = (exp_s * jnp.exp(max_s - lse_s) * (gap - mean)).astype(bf16)
    out_ref[...] = lax.dot_general(
        hit_bf16, gradient, (((0,), (0,)), ((), ())), preferred_element_type=f32
    ).astype(bf16)
    own_row = lax.broadcasted_iota(jnp.int32, (rows, local_tokens), 0) - d * LIVE
    own = (own_row == own_slot) & (own_slot >= 0)
    div_ref[...] = jnp.sum(jnp.where(own, kl, 0.0), axis=0, keepdims=True)
    ratio_ref[...] = jnp.sum(jnp.where(own, ratio, 0.0), axis=0, keepdims=True)


def on_device(
    teacher_hidden,
    student_hidden,
    teacher_head,
    student_head,
    teacher_gain,
    lengths,
    student_row,
    targets,
):
    n_dp = lax.axis_size("dp")
    n_t = lax.axis_size("tensor")
    local_tokens, width_t = teacher_hidden.shape
    width_s = student_hidden.shape[1]
    tokens = local_tokens * n_dp
    vocab = teacher_head.shape[1]
    rows = n_dp * LIVE
    half = n_t // 2
    n_dev = n_dp * n_t
    bf16, f32 = jnp.bfloat16, jnp.float32
    dma = pltpu.SemaphoreType.DMA
    hbm = pl.BlockSpec(memory_space=pl.ANY)
    vmem = pl.BlockSpec(memory_space=pltpu.VMEM)
    gradient, divergence, log_ratio = pl.pallas_call(
        functools.partial(kernel, n_dp, n_t),
        out_shape=(
            jax.ShapeDtypeStruct((tokens, vocab), bf16),
            jax.ShapeDtypeStruct((1, local_tokens), f32),
            jax.ShapeDtypeStruct((1, local_tokens), f32),
        ),
        in_specs=[hbm] * 8,
        out_specs=(vmem,) * 3,
        scratch_shapes=[
            pltpu.VMEM((local_tokens, width_t), bf16),
            pltpu.VMEM(teacher_head.shape, bf16),
            pltpu.VMEM(student_head.shape, bf16),
            pltpu.VMEM((n_t, 1, width_t), f32),
            pltpu.SMEM(lengths.shape, jnp.int32),
            pltpu.VMEM((1, tokens), jnp.int32),
            pltpu.VMEM((1, tokens), jnp.int32),
            pltpu.VMEM((n_t, n_dp, LIVE, width_t), bf16),
            pltpu.VMEM((n_dp, local_tokens, width_s), bf16),
            pltpu.VMEM((n_t, rows, width_s), bf16),
            pltpu.VMEM((1, 4 * rows), f32),
            pltpu.VMEM((n_dev, 1, 4 * rows), f32),
            dma((8,)),
            *[dma((n_dp,))] * 4,
            *[dma((half,))] * 8,
            *[dma((n_dev,))] * 2,
        ],
        compiler_params=pltpu.CompilerParams(collective_id=0, has_side_effects=True),
    )(
        teacher_hidden,
        student_hidden,
        teacher_head,
        student_head,
        teacher_gain.reshape(n_t, 1, width_t),
        lengths,
        student_row.reshape(1, tokens),
        targets.reshape(1, tokens),
    )
    return gradient, divergence.reshape(local_tokens), log_ratio.reshape(local_tokens)


def solution(mesh):
    return jax.shard_map(
        on_device,
        mesh=mesh,
        in_specs=(
            P("dp", "tensor"),
            P("dp", "tensor"),
            P(None, ("dp", "tensor")),
            P(None, ("dp", "tensor")),
            P(),
            P(),
            P(),
            P(),
        ),
        out_specs=(P(None, ("dp", "tensor")), P("dp"), P("dp")),
        check_vma=False,
    )
```

```python
import functools

import jax
import jax.numpy as jnp
from jax import lax
from jax.experimental import pallas as pl
from jax.experimental.pallas import tpu as pltpu
from jax.sharding import PartitionSpec as P

LIVE = 8
MESH = pl.DeviceIdType.MESH


def kernel(
    n_dp,
    n_t,
    th_hbm,
    sh_hbm,
    thead_hbm,
    shead_hbm,
    gain_hbm,
    len_hbm,
    srow_hbm,
    tgt_hbm,
    out_ref,
    div_ref,
    ratio_ref,
    th,
    thead,
    shead,
    gain,
    lens,
    srow,
    tgt,
    tg,
    sz,
    sg,
    mine,
    stats,
    local_sem,
    zt_send,
    zt_recv,
    zs_send,
    zs_recv,
    xt_send,
    xt_recv,
    xs_send,
    xs_recv,
    pt_send,
    pt_recv,
    ps_send,
    ps_recv,
    st_send,
    st_recv,
):
    f32, bf16 = jnp.float32, jnp.bfloat16
    d = lax.axis_index("dp")
    t = lax.axis_index("tensor")
    half = n_t // 2
    chip, core = t // 2, t % 2
    partner = chip * 2 + 1 - core
    local_tokens, width_t = th_hbm.shape
    width_s = sh_hbm.shape[1]
    tokens = local_tokens * n_dp
    seqs = lens.shape[0]
    seq_dev = seqs // n_dp
    slot = tokens // seqs
    vocab = thead.shape[1]
    rows = n_dp * LIVE
    lanes = 4 * rows
    n_dev = n_dp * n_t

    local = [
        pltpu.make_async_copy(src, dst, local_sem.at[i])
        for i, (src, dst) in enumerate(
            [
                (len_hbm, lens),
                (th_hbm, th),
                (sh_hbm, sz.at[d]),
                (srow_hbm, srow),
                (tgt_hbm, tgt),
                (gain_hbm, gain),
                (shead_hbm, shead),
                (thead_hbm, thead),
            ]
        )
    ]
    for copy in local:
        copy.start()

    def dp_peer(k):
        return lax.rem(d + k, n_dp)

    def chip_peer(k):
        return lax.rem(chip + k, half) * 2 + core

    barrier = pltpu.get_barrier_semaphore()
    for k in range(1, n_dp):
        pl.semaphore_signal(barrier, inc=1, device_id=(dp_peer(k), t), device_id_type=MESH)
    for k in range(1, half):
        pl.semaphore_signal(barrier, inc=1, device_id=(d, chip_peer(k)), device_id_type=MESH)
    pl.semaphore_signal(barrier, inc=1, device_id=(d, partner), device_id_type=MESH)

    local[0].wait()
    lane = lax.broadcasted_iota(jnp.int32, (1, local_tokens), 1)
    own_slot = jnp.full((1, local_tokens), -1, jnp.int32)
    offset = jnp.int32(0)
    for q in range(seq_dev):
        length = lens[d * seq_dev + q]
        pos = lane - q * slot
        own_slot = jnp.where((pos >= 0) & (pos < length), pos + offset, own_slot)
        offset = offset + length
    own_hit = lax.broadcasted_iota(jnp.int32, (LIVE, local_tokens), 0) == own_slot
    local[1].wait()
    tg[t, d] = jnp.dot(
        jnp.where(own_hit, 1.0, 0.0).astype(bf16), th[...], preferred_element_type=f32
    ).astype(bf16)
    local[2].wait()

    pl.semaphore_wait(barrier, n_dp - 1 + half - 1 + 1)

    def remote(src, dst, send, recv, device):
        return pltpu.make_async_remote_copy(
            src_ref=src, dst_ref=dst, send_sem=send, recv_sem=recv, device_id=device, device_id_type=MESH
        )

    upper = (2 * d) // n_dp
    order = [upper * m + (1 - upper) * (n_dp - m) for m in range(1, n_dp)]
    z_s = [
        remote(sz.at[d], sz.at[d], zs_send.at[k], zs_recv.at[k], (dp_peer(k), t)) for k in order
    ]
    z_t = [
        remote(tg.at[t, d], tg.at[t, d], zt_send.at[k], zt_recv.at[k], (dp_peer(k), t))
        for k in order
    ]
    for copy in z_s + z_t:
        copy.start()
    started = z_s + z_t

    def spread(j):
        piece = tg.at[t, lax.rem(d - j + n_dp, n_dp)]
        copies = [
            remote(piece, piece, xt_send.at[k, j], xt_recv.at[k, j], (d, chip_peer(k)))
            for k in range(1, half)
        ]
        for copy in copies:
            copy.start()
        return copies

    x_t = [spread(0)]

    local[3].wait()
    local[4].wait()
    token = lax.broadcasted_iota(jnp.int32, (1, tokens), 1)
    slot_of = jnp.full((1, tokens), -1, jnp.int32)
    for s in range(seqs):
        if s % seq_dev == 0:
            offset = jnp.int32(s // seq_dev * LIVE)
        length = lens[s]
        pos = token - s * slot
        slot_of = jnp.where((pos >= 0) & (pos < length), pos + offset, slot_of)
        offset = offset + length
    row = lax.broadcasted_iota(jnp.int32, (rows, tokens), 0)
    hit = row == slot_of
    hit_bf16 = jnp.where(hit, 1.0, 0.0).astype(bf16)
    source = jnp.sum(jnp.where(hit, srow[...].astype(f32), 0.0), axis=1, keepdims=True)
    wanted = jnp.sum(jnp.where(hit, tgt[...].astype(f32), 0.0), axis=1, keepdims=True)
    pick = lax.broadcasted_iota(jnp.int32, (rows, tokens), 1) == source.astype(jnp.int32)
    pick_bf16 = jnp.where(pick, 1.0, 0.0).astype(bf16)

    for copy in z_s:
        copy.wait_recv()
    everyone = sz[...].reshape(tokens, width_s)
    sg[t] = jnp.dot(pick_bf16, everyone, preferred_element_type=f32).astype(bf16)
    x_s = [
        remote(sg.at[t], sg.at[t], xs_send.at[k], xs_recv.at[k], (d, chip_peer(k)))
        for k in range(1, half)
    ]
    p_s = [remote(sg.at[t], sg.at[t], ps_send.at[0], ps_recv.at[0], (d, partner))]
    for copy in x_s + p_s:
        copy.start()

    for j, copy in zip(order, z_t):
        copy.wait_recv()
        x_t.append(spread(j))
    p_t = [remote(tg.at[t], tg.at[t], pt_send.at[0], pt_recv.at[0], (d, partner))]
    p_t[0].start()

    for copy in local[5:]:
        copy.wait()

    square = jnp.zeros((rows, 1), f32)
    acc_t = jnp.zeros((2 * rows, vocab), f32)
    acc_s = jnp.zeros((rows, vocab), f32)

    def add_t(which, square, acc_t):
        x = tg[which].astype(f32).reshape(rows, width_t)
        square = square + jnp.sum(x * x, axis=1, keepdims=True)
        x = x * gain[which]
        high = x.astype(bf16)
        low = (x - high.astype(f32)).astype(bf16)
        at_t = pl.ds(pl.multiple_of(which * width_t, width_t), width_t)
        acc_t = acc_t + jnp.dot(
            jnp.concatenate([high, low], axis=0), thead[at_t, :], preferred_element_type=f32
        )
        return square, acc_t

    def add_s(which, acc_s):
        at_s = pl.ds(pl.multiple_of(which * width_s, width_s), width_s)
        return acc_s + jnp.dot(sg[which], shead[at_s, :], preferred_element_type=f32)

    same = [lax.rem(chip - k + half, half) * 2 + core for k in range(half)]
    other = [lax.rem(chip - k + half, half) * 2 + 1 - core for k in range(half)]
    square, acc_t = add_t(t, square, acc_t)
    acc_s = add_s(t, acc_s)
    for k in range(1, half):
        for j, copies in zip([0] + order, x_t):
            copies[k - 1].wait_recv()
        block = tg.at[same[k]]
        p_t.append(remote(block, block, pt_send.at[k], pt_recv.at[k], (d, partner)))
        p_t[k].start()
        x_s[k - 1].wait_recv()
        block = sg.at[same[k]]
        p_s.append(remote(block, block, ps_send.at[k], ps_recv.at[k], (d, partner)))
        p_s[k].start()
        square, acc_t = add_t(same[k], square, acc_t)
        acc_s = add_s(same[k], acc_s)
    for k in range(half):
        p_t[k].wait_recv()
        p_s[k].wait_recv()
        square, acc_t = add_t(other[k], square, acc_t)
        acc_s = add_s(other[k], acc_s)
    for copies in x_t:
        started += copies
    started += x_s + p_t + p_s

    scale = lax.rsqrt(square / (width_t * n_t) + 1e-06)
    logits_t = (acc_t[:rows] + acc_t[rows:]) * scale
    gap = acc_s - logits_t
    max_t = jnp.max(logits_t, axis=1, keepdims=True)
    max_s = jnp.max(acc_s, axis=1, keepdims=True)
    sum_t = jnp.sum(jnp.exp(logits_t - max_t), axis=1, keepdims=True)
    exp_s = jnp.exp(acc_s - max_s)
    sum_s = jnp.sum(exp_s, axis=1, keepdims=True)
    cross = jnp.sum(exp_s * gap, axis=1, keepdims=True) / sum_s
    me = d * n_t + t
    column = lax.broadcasted_iota(jnp.int32, (rows, vocab), 1) + me * vocab
    chosen = jnp.sum(
        jnp.where(column == wanted.astype(jnp.int32), gap, 0.0), axis=1, keepdims=True
    )

    place = lax.broadcasted_iota(jnp.int32, (rows, lanes), 1) - lax.broadcasted_iota(
        jnp.int32, (rows, lanes), 0
    )
    packed = jnp.zeros((rows, lanes), f32)
    for i, value in enumerate((max_t + jnp.log(sum_t), max_s + jnp.log(sum_s), cross, chosen)):
        packed = jnp.where(place == i * rows, value, packed)
    mine[...] = jnp.sum(packed, axis=0, keepdims=True)
    stats[me] = mine[...]

    def stat(d_to, t_to):
        remote(mine, stats.at[me], st_send.at[0], st_recv.at[0], (d_to, t_to)).start()

    others = [lax.rem(t + j, n_t) for j in range(n_t)]

    def start(m, carry):
        d_to = dp_peer(upper * m + (1 - upper) * (n_dp - m))
        for t_to in others:
            stat(d_to, t_to)
        return carry

    lax.fori_loop(1, n_dp, start, 0, unroll=n_dp <= 4)
    for t_to in others[1:]:
        stat(d, t_to)
    for copy in started:
        copy.wait_send()
    rest = stats.at[pl.ds(0, n_dev - 1)]
    remote(rest, rest, st_send.at[0], st_recv.at[0], (d, partner)).wait()

    table = stats[...].reshape(n_dev, lanes)
    top = jnp.max(table, axis=0, keepdims=True)
    weight = jnp.exp(table - top)
    total = jnp.sum(weight, axis=0, keepdims=True)
    lse = top + jnp.log(total)
    moved = pltpu.roll(weight, rows, 1)
    mean_gap = jnp.sum(table * moved, axis=0, keepdims=True) / jnp.sum(moved, axis=0, keepdims=True)
    target_gap = jnp.sum(table, axis=0, keepdims=True)

    def per_slot(value, i):
        return jnp.sum(jnp.where(place == i * rows, value, 0.0), axis=1, keepdims=True)

    lse_t, lse_s = per_slot(lse, 0), per_slot(lse, 1)
    mean = per_slot(mean_gap, 2)
    ratio = per_slot(target_gap, 3) - lse_s + lse_t
    kl = mean - lse_s + lse_t
    gradient = (exp_s * jnp.exp(max_s - lse_s) * (gap - mean)).astype(bf16)
    out_ref[...] = lax.dot_general(
        hit_bf16, gradient, (((0,), (0,)), ((), ())), preferred_element_type=f32
    ).astype(bf16)
    own_row = lax.broadcasted_iota(jnp.int32, (rows, local_tokens), 0) - d * LIVE
    own = (own_row == own_slot) & (own_slot >= 0)
    div_ref[...] = jnp.sum(jnp.where(own, kl, 0.0), axis=0, keepdims=True)
    ratio_ref[...] = jnp.sum(jnp.where(own, ratio, 0.0), axis=0, keepdims=True)


def write_out(a, b, c, a_out, b_out, c_out, sem):
    copies = [
        pltpu.make_async_copy(src, dst, sem.at[i])
        for i, (src, dst) in enumerate([(a, a_out), (b, b_out), (c, c_out)])
    ]
    for copy in copies:
        copy.start()
    for copy in copies:
        copy.wait()


def on_device(
    teacher_hidden,
    student_hidden,
    teacher_head,
    student_head,
    teacher_gain,
    lengths,
    student_row,
    targets,
):
    n_dp = lax.axis_size("dp")
    n_t = lax.axis_size("tensor")
    local_tokens, width_t = teacher_hidden.shape
    width_s = student_hidden.shape[1]
    tokens = local_tokens * n_dp
    vocab = teacher_head.shape[1]
    rows = n_dp * LIVE
    half = n_t // 2
    n_dev = n_dp * n_t
    bf16, f32 = jnp.bfloat16, jnp.float32
    dma = pltpu.SemaphoreType.DMA
    hbm = pl.BlockSpec(memory_space=pl.ANY)
    vmem = pl.BlockSpec(memory_space=pltpu.VMEM)
    gradient, divergence, log_ratio = pl.pallas_call(
        functools.partial(kernel, n_dp, n_t),
        out_shape=(
            pltpu.VMEM((tokens, vocab), bf16),
            pltpu.VMEM((1, local_tokens), f32),
            pltpu.VMEM((1, local_tokens), f32),
        ),
        in_specs=[hbm] * 8,
        out_specs=(vmem,) * 3,
        scratch_shapes=[
            pltpu.VMEM((local_tokens, width_t), bf16),
            pltpu.VMEM(teacher_head.shape, bf16),
            pltpu.VMEM(student_head.shape, bf16),
            pltpu.VMEM((n_t, 1, width_t), f32),
            pltpu.SMEM(lengths.shape, jnp.int32),
            pltpu.VMEM((1, tokens), jnp.int32),
            pltpu.VMEM((1, tokens), jnp.int32),
            pltpu.VMEM((n_t, n_dp, LIVE, width_t), bf16),
            pltpu.VMEM((n_dp, local_tokens, width_s), bf16),
            pltpu.VMEM((n_t, rows, width_s), bf16),
            pltpu.VMEM((1, 4 * rows), f32),
            pltpu.VMEM((n_dev, 1, 4 * rows), f32),
            dma((8,)),
            *[dma((n_dp,))] * 4,
            *[dma((half, n_dp))] * 2,
            *[dma((half,))] * 6,
            *[dma((1,))] * 2,
        ],
        compiler_params=pltpu.CompilerParams(collective_id=0, has_side_effects=True),
    )(
        teacher_hidden,
        student_hidden,
        teacher_head,
        student_head,
        teacher_gain.reshape(n_t, 1, width_t),
        lengths,
        student_row.reshape(1, tokens),
        targets.reshape(1, tokens),
    )
    gradient, divergence, log_ratio = pl.pallas_call(
        write_out,
        out_shape=(
            jax.ShapeDtypeStruct((tokens, vocab), bf16),
            jax.ShapeDtypeStruct((1, local_tokens), f32),
            jax.ShapeDtypeStruct((1, local_tokens), f32),
        ),
        in_specs=[vmem] * 3,
        out_specs=(hbm,) * 3,
        scratch_shapes=[dma((3,))],
    )(*[pltpu.with_memory_space_constraint(x, pltpu.VMEM) for x in (gradient, divergence, log_ratio)])
    return gradient, divergence.reshape(local_tokens), log_ratio.reshape(local_tokens)


def solution(mesh):
    return jax.shard_map(
        on_device,
        mesh=mesh,
        in_specs=(
            P("dp", "tensor"),
            P("dp", "tensor"),
            P(None, ("dp", "tensor")),
            P(None, ("dp", "tensor")),
            P(),
            P(),
            P(),
            P(),
        ),
        out_specs=(P(None, ("dp", "tensor")), P("dp"), P("dp")),
        check_vma=False,
    )
```

```python
import functools

import jax
import jax.numpy as jnp
from jax import lax
from jax.experimental import pallas as pl
from jax.experimental.pallas import tpu as pltpu
from jax.sharding import PartitionSpec as P

LIVE = 8
MESH = pl.DeviceIdType.MESH


def kernel(
    n_dp,
    n_t,
    th_hbm,
    sh_hbm,
    thead_hbm,
    shead_hbm,
    gain_hbm,
    len_hbm,
    srow_hbm,
    tgt_hbm,
    out_ref,
    div_ref,
    ratio_ref,
    th,
    thead,
    shead,
    gain,
    lens,
    srow,
    tgt,
    tg,
    sz,
    sg,
    mine,
    stats,
    local_sem,
    zt_send,
    zt_recv,
    zs_send,
    zs_recv,
    xt_send,
    xt_recv,
    xs_send,
    xs_recv,
    pt_send,
    pt_recv,
    ps_send,
    ps_recv,
    st_send,
    st_recv,
):
    f32, bf16 = jnp.float32, jnp.bfloat16
    d = lax.axis_index("dp")
    t = lax.axis_index("tensor")
    half = n_t // 2
    chip, core = t // 2, t % 2
    partner = chip * 2 + 1 - core
    local_tokens, width_t = th_hbm.shape
    width_s = sh_hbm.shape[1]
    tokens = local_tokens * n_dp
    seqs = lens.shape[0]
    seq_dev = seqs // n_dp
    slot = tokens // seqs
    vocab = thead.shape[1]
    rows = n_dp * LIVE
    lanes = 4 * rows
    n_dev = n_dp * n_t

    def dp_peer(k):
        return lax.rem(d + k, n_dp)

    turn = lax.rem(2 * half - 1 - 2 * chip + half * half, half)

    def chip_at(k):
        return lax.rem(chip + turn * k, half)

    def chip_peer(k):
        return chip_at(k) * 2 + core

    barrier = pltpu.get_barrier_semaphore()
    upper = (2 * d) // n_dp
    order = [upper * m + (1 - upper) * (n_dp - m) for m in range(1, n_dp)]
    for k in order:
        pl.semaphore_signal(barrier, inc=1, device_id=(dp_peer(k), t), device_id_type=MESH)
    for k in range(1, half):
        pl.semaphore_signal(barrier, inc=1, device_id=(d, chip_peer(k)), device_id_type=MESH)
    pl.semaphore_signal(barrier, inc=1, device_id=(d, partner), device_id_type=MESH)

    local = [
        pltpu.make_async_copy(src, dst, local_sem.at[i])
        for i, (src, dst) in enumerate(
            [
                (len_hbm, lens),
                (th_hbm, th),
                (sh_hbm, sz.at[d]),
                (srow_hbm, srow),
                (tgt_hbm, tgt),
                (gain_hbm, gain),
                (shead_hbm, shead),
                (thead_hbm, thead),
            ]
        )
    ]
    for copy in local:
        copy.start()

    local[0].wait()
    lane = lax.broadcasted_iota(jnp.int32, (1, local_tokens), 1)
    own_slot = jnp.full((1, local_tokens), -1, jnp.int32)
    offset = jnp.int32(0)
    for q in range(seq_dev):
        length = lens[d * seq_dev + q]
        pos = lane - q * slot
        own_slot = jnp.where((pos >= 0) & (pos < length), pos + offset, own_slot)
        offset = offset + length
    own_hit = lax.broadcasted_iota(jnp.int32, (LIVE, local_tokens), 0) == own_slot
    local[1].wait()
    tg[t, d] = jnp.dot(
        jnp.where(own_hit, 1.0, 0.0).astype(bf16), th[...], preferred_element_type=f32
    ).astype(bf16)
    local[2].wait()

    pl.semaphore_wait(barrier, n_dp - 1 + half - 1 + 1)

    def remote(src, dst, send, recv, device):
        return pltpu.make_async_remote_copy(
            src_ref=src, dst_ref=dst, send_sem=send, recv_sem=recv, device_id=device, device_id_type=MESH
        )

    z_s = [
        remote(sz.at[d], sz.at[d], zs_send.at[k], zs_recv.at[k], (dp_peer(k), t)) for k in order
    ]
    z_t = [
        remote(tg.at[t, d], tg.at[t, d], zt_send.at[k], zt_recv.at[k], (dp_peer(k), t))
        for k in order
    ]
    for copy in z_s + z_t:
        copy.start()
    started = z_s + z_t

    def spread(j):
        piece = tg.at[t, lax.rem(d - j + n_dp, n_dp)]
        copies = [
            remote(piece, piece, xt_send.at[k, j], xt_recv.at[chip, j], (d, chip_peer(k)))
            for k in range(1, half)
        ]
        for copy in copies:
            copy.start()
        return copies

    x_t = [spread(0)]

    local[3].wait()
    local[4].wait()
    token = lax.broadcasted_iota(jnp.int32, (1, tokens), 1)
    slot_of = jnp.full((1, tokens), -1, jnp.int32)
    for s in range(seqs):
        if s % seq_dev == 0:
            offset = jnp.int32(s // seq_dev * LIVE)
        length = lens[s]
        pos = token - s * slot
        slot_of = jnp.where((pos >= 0) & (pos < length), pos + offset, slot_of)
        offset = offset + length
    row = lax.broadcasted_iota(jnp.int32, (rows, tokens), 0)
    hit = row == slot_of
    hit_bf16 = jnp.where(hit, 1.0, 0.0).astype(bf16)
    source = jnp.sum(jnp.where(hit, srow[...].astype(f32), 0.0), axis=1, keepdims=True)
    wanted = jnp.sum(jnp.where(hit, tgt[...].astype(f32), 0.0), axis=1, keepdims=True)
    pick = lax.broadcasted_iota(jnp.int32, (rows, tokens), 1) == source.astype(jnp.int32)
    pick_bf16 = jnp.where(pick, 1.0, 0.0).astype(bf16)

    for j, copy in zip(order[:-1], z_t[:-1]):
        copy.wait_recv()
        x_t.append(spread(j))

    for copy in z_s:
        copy.wait_recv()
    everyone = sz[...].reshape(tokens, width_s)
    sg[t] = jnp.dot(pick_bf16, everyone, preferred_element_type=f32).astype(bf16)
    x_s = [
        remote(sg.at[t], sg.at[t], xs_send.at[k], xs_recv.at[chip], (d, chip_peer(k)))
        for k in range(1, half)
    ]
    p_s = [remote(sg.at[t], sg.at[t], ps_send.at[0], ps_recv.at[0], (d, partner))]
    for copy in x_s + p_s:
        copy.start()

    z_t[-1].wait_recv()
    x_t.append(spread(order[-1]))
    p_t = [remote(tg.at[t], tg.at[t], pt_send.at[0], pt_recv.at[0], (d, partner))]
    p_t[0].start()

    for copy in local[5:]:
        copy.wait()

    square = jnp.zeros((rows, 1), f32)
    acc_t = jnp.zeros((2 * rows, vocab), f32)
    acc_s = jnp.zeros((rows, vocab), f32)

    def add_t(which, square, acc_t):
        x = tg[which].astype(f32).reshape(rows, width_t)
        square = square + jnp.sum(x * x, axis=1, keepdims=True)
        x = x * gain[which]
        high = x.astype(bf16)
        low = (x - high.astype(f32)).astype(bf16)
        at_t = pl.ds(pl.multiple_of(which * width_t, width_t), width_t)
        acc_t = acc_t + jnp.dot(
            jnp.concatenate([high, low], axis=0), thead[at_t, :], preferred_element_type=f32
        )
        return square, acc_t

    def add_s(which, acc_s):
        at_s = pl.ds(pl.multiple_of(which * width_s, width_s), width_s)
        return acc_s + jnp.dot(sg[which], shead[at_s, :], preferred_element_type=f32)

    square, acc_t = add_t(t, square, acc_t)
    acc_s = add_s(t, acc_s)
    pieces = [0] + order
    for k in range(1, half):
        origin = chip_at(half - k)
        block = tg.at[origin * 2 + core]
        for j in pieces:
            piece = tg.at[origin * 2 + core, lax.rem(d - j + n_dp, n_dp)]
            remote(
                piece, piece, xt_send.at[k, j], xt_recv.at[origin, j], (d, partner)
            ).wait_recv()
        p_t.append(remote(block, block, pt_send.at[k], pt_recv.at[k], (d, partner)))
        p_t[k].start()
        block = sg.at[origin * 2 + core]
        remote(block, block, xs_send.at[k], xs_recv.at[origin], (d, partner)).wait_recv()
        p_s.append(remote(block, block, ps_send.at[k], ps_recv.at[k], (d, partner)))
        p_s[k].start()
        square, acc_t = add_t(origin * 2 + core, square, acc_t)
        acc_s = add_s(origin * 2 + core, acc_s)
    for k in range(half):
        origin = chip_at(half - k) if k else chip
        p_t[k].wait_recv()
        p_s[k].wait_recv()
        square, acc_t = add_t(origin * 2 + 1 - core, square, acc_t)
        acc_s = add_s(origin * 2 + 1 - core, acc_s)
    for copies in x_t:
        started += copies
    started += x_s + p_t + p_s

    scale = lax.rsqrt(square / (width_t * n_t) + 1e-06)
    logits_t = (acc_t[:rows] + acc_t[rows:]) * scale
    gap = acc_s - logits_t
    max_t = jnp.max(logits_t, axis=1, keepdims=True)
    max_s = jnp.max(acc_s, axis=1, keepdims=True)
    sum_t = jnp.sum(jnp.exp(logits_t - max_t), axis=1, keepdims=True)
    exp_s = jnp.exp(acc_s - max_s)
    sum_s = jnp.sum(exp_s, axis=1, keepdims=True)
    cross = jnp.sum(exp_s * gap, axis=1, keepdims=True) / sum_s
    me = d * n_t + t
    column = lax.broadcasted_iota(jnp.int32, (rows, vocab), 1) + me * vocab
    chosen = jnp.sum(
        jnp.where(column == wanted.astype(jnp.int32), gap, 0.0), axis=1, keepdims=True
    )

    place = lax.broadcasted_iota(jnp.int32, (rows, lanes), 1) - lax.broadcasted_iota(
        jnp.int32, (rows, lanes), 0
    )
    packed = jnp.zeros((rows, lanes), f32)
    for i, value in enumerate((max_t + jnp.log(sum_t), max_s + jnp.log(sum_s), cross, chosen)):
        packed = jnp.where(place == i * rows, value, packed)
    mine[...] = jnp.sum(packed, axis=0, keepdims=True)
    stats[me] = mine[...]

    def stat(d_to, t_to):
        remote(mine, stats.at[me], st_send.at[0], st_recv.at[0], (d_to, t_to)).start()

    others = [lax.rem(t + j, n_t) for j in range(n_t)]

    def start(m, carry):
        d_to = dp_peer(upper * m + (1 - upper) * (n_dp - m))
        for t_to in others:
            stat(d_to, t_to)
        return carry

    lax.fori_loop(1, n_dp, start, 0, unroll=n_dp <= 4)
    for t_to in others[1:]:
        stat(d, t_to)
    for copy in started:
        copy.wait_send()
    rest = stats.at[pl.ds(0, n_dev - 1)]
    remote(rest, rest, st_send.at[0], st_recv.at[0], (d, partner)).wait()

    table = stats[...].reshape(n_dev, lanes)
    top = jnp.max(table, axis=0, keepdims=True)
    weight = jnp.exp(table - top)
    total = jnp.sum(weight, axis=0, keepdims=True)
    lse = top + jnp.log(total)
    moved = pltpu.roll(weight, rows, 1)
    mean_gap = jnp.sum(table * moved, axis=0, keepdims=True) / jnp.sum(moved, axis=0, keepdims=True)
    target_gap = jnp.sum(table, axis=0, keepdims=True)

    def per_slot(value, i):
        return jnp.sum(jnp.where(place == i * rows, value, 0.0), axis=1, keepdims=True)

    lse_t, lse_s = per_slot(lse, 0), per_slot(lse, 1)
    mean = per_slot(mean_gap, 2)
    ratio = per_slot(target_gap, 3) - lse_s + lse_t
    kl = mean - lse_s + lse_t
    gradient = (exp_s * jnp.exp(max_s - lse_s) * (gap - mean)).astype(bf16)
    out_ref[...] = lax.dot_general(
        hit_bf16, gradient, (((0,), (0,)), ((), ())), preferred_element_type=f32
    ).astype(bf16)
    own_row = lax.broadcasted_iota(jnp.int32, (rows, local_tokens), 0) - d * LIVE
    own = (own_row == own_slot) & (own_slot >= 0)
    div_ref[...] = jnp.sum(jnp.where(own, kl, 0.0), axis=0, keepdims=True)
    ratio_ref[...] = jnp.sum(jnp.where(own, ratio, 0.0), axis=0, keepdims=True)


def write_out(a, b, c, a_out, b_out, c_out, sem):
    copies = [
        pltpu.make_async_copy(src, dst, sem.at[i])
        for i, (src, dst) in enumerate([(a, a_out), (b, b_out), (c, c_out)])
    ]
    for copy in copies:
        copy.start()
    for copy in copies:
        copy.wait()


def on_device(
    teacher_hidden,
    student_hidden,
    teacher_head,
    student_head,
    teacher_gain,
    lengths,
    student_row,
    targets,
):
    n_dp = lax.axis_size("dp")
    n_t = lax.axis_size("tensor")
    local_tokens, width_t = teacher_hidden.shape
    width_s = student_hidden.shape[1]
    tokens = local_tokens * n_dp
    vocab = teacher_head.shape[1]
    rows = n_dp * LIVE
    half = n_t // 2
    n_dev = n_dp * n_t
    bf16, f32 = jnp.bfloat16, jnp.float32
    dma = pltpu.SemaphoreType.DMA
    hbm = pl.BlockSpec(memory_space=pl.ANY)
    vmem = pl.BlockSpec(memory_space=pltpu.VMEM)
    gradient, divergence, log_ratio = pl.pallas_call(
        functools.partial(kernel, n_dp, n_t),
        out_shape=(
            pltpu.VMEM((tokens, vocab), bf16),
            pltpu.VMEM((1, local_tokens), f32),
            pltpu.VMEM((1, local_tokens), f32),
        ),
        in_specs=[hbm] * 8,
        out_specs=(vmem,) * 3,
        scratch_shapes=[
            pltpu.VMEM((local_tokens, width_t), bf16),
            pltpu.VMEM(teacher_head.shape, bf16),
            pltpu.VMEM(student_head.shape, bf16),
            pltpu.VMEM((n_t, 1, width_t), f32),
            pltpu.SMEM(lengths.shape, jnp.int32),
            pltpu.VMEM((1, tokens), jnp.int32),
            pltpu.VMEM((1, tokens), jnp.int32),
            pltpu.VMEM((n_t, n_dp, LIVE, width_t), bf16),
            pltpu.VMEM((n_dp, local_tokens, width_s), bf16),
            pltpu.VMEM((n_t, rows, width_s), bf16),
            pltpu.VMEM((1, 4 * rows), f32),
            pltpu.VMEM((n_dev, 1, 4 * rows), f32),
            dma((8,)),
            *[dma((n_dp,))] * 4,
            *[dma((half, n_dp))] * 2,
            *[dma((half,))] * 6,
            *[dma((1,))] * 2,
        ],
        compiler_params=pltpu.CompilerParams(collective_id=0, has_side_effects=True),
    )(
        teacher_hidden,
        student_hidden,
        teacher_head,
        student_head,
        teacher_gain.reshape(n_t, 1, width_t),
        lengths,
        student_row.reshape(1, tokens),
        targets.reshape(1, tokens),
    )
    gradient, divergence, log_ratio = pl.pallas_call(
        write_out,
        out_shape=(
            jax.ShapeDtypeStruct((tokens, vocab), bf16),
            jax.ShapeDtypeStruct((1, local_tokens), f32),
            jax.ShapeDtypeStruct((1, local_tokens), f32),
        ),
        in_specs=[vmem] * 3,
        out_specs=(hbm,) * 3,
        scratch_shapes=[dma((3,))],
    )(*[pltpu.with_memory_space_constraint(x, pltpu.VMEM) for x in (gradient, divergence, log_ratio)])
    return gradient, divergence.reshape(local_tokens), log_ratio.reshape(local_tokens)


def solution(mesh):
    return jax.shard_map(
        on_device,
        mesh=mesh,
        in_specs=(
            P("dp", "tensor"),
            P("dp", "tensor"),
            P(None, ("dp", "tensor")),
            P(None, ("dp", "tensor")),
            P(),
            P(),
            P(),
            P(),
        ),
        out_specs=(P(None, ("dp", "tensor")), P("dp"), P("dp")),
        check_vma=False,
    )
```
